512 devices in a mesh: inst: 16 (over z), mesh: 32 (over y, x, core).
Axes of the slice: x: 4, y: 4, z: 16, core: 2. Of those that a mesh axis runs over, the one named last changes fastest.
Arguments:
- state: float32 [16, 6, 2048, 128], P('inst', None, 'mesh'), may hold values from -6 to 6
- right_side: float32 [16, 6, 2048, 128], P('inst', None, 'mesh'), may hold values from -6 to 6
- couplings: float32 [3, 16, 6, 2048, 128], P(None, 'inst', None, 'mesh'), may hold values from 0.05 to 0.35
- jac_corr: float32 [16, 6, 6, 2048, 128], P('inst', None, None, 'mesh'), may hold values from -0.3 to 0.3
- spec_scale: float32 [2048, 128], P('mesh'), may hold values from 0.005 to 0.05
- row_id: int32 [2048], P('mesh'), may hold values from 0 to 2
- send_index: int32 [1024, 2], P('mesh'), may hold values from 0 to 63
- recv_slot: int32 [2048], P('mesh'), may hold values from 0 to 63, as said below
- iface_coef: float32 [64, 128], P('mesh'), may hold values from 0.2 to 0.6
- donor_index: int32 [64, 2], P('mesh'), may hold values from 0 to 63
- donor_weight: float32 [64, 2], P('mesh'), may hold values from 0.2 to 1
- phase_shift: int32 [64], P('mesh'), may hold values from 0 to 15
Outputs:
- smoothed: float32 [16, 6, 2048, 128], P('inst', None, 'mesh')
The draws below stay inside these ranges and needn't reach their ends.
Inputs may be any that keep to these rules, and one draw needn't show every extreme that they name: `recv_slot`: among the 64 blocks of each mesh index, every slot 0 to 32 * 2 - 1 is named by at least one block.
All inputs are finite; a program needn't handle non-finite values.
Results may differ from the reference program's by a relative error of at most 0.0001.
Values sent between devices are 32-bit elements; how exact they have to be, the bound alone decides.
No kernel may reach another device: no remote copies, remote signals or barrier semaphores. Data moves between devices by JAX's collectives and lax.ppermute only.
A program may use at most 64 MiB of HBM per device.

```python
import math
import jax
import jax.numpy as jnp
from jax import lax

NT = 16
NV = 6
BLOCK_CELLS = 128
BLK_DEV = 64
HALO_SLOTS = 2
IF_DEV = 2
SWEEPS = 2
NB = 2048
IFACE = 64
N_MESH = 32


def draw_recv_slot(key, part):
    device_keys = jax.random.split(jax.random.fold_in(key, 7), N_MESH)

    def one_device(device_key):
        order = jax.random.permutation(device_key, jnp.arange(BLK_DEV, dtype=jnp.int32))
        return (order % (N_MESH * HALO_SLOTS)).astype(jnp.int32)
    return jax.vmap(one_device)(device_keys).reshape(-1).astype(jnp.int32)


def draw_donor_index(key, part):
    picks = jax.random.randint(jax.random.fold_in(key, 11), (IFACE, 2), 0, IFACE).astype(jnp.int32)
    picks = picks.at[0, 0].set(0)
    return picks.at[0, 1].set(N_MESH // 2 * IF_DEV).astype(jnp.int32)


def draw_phase_shift(key, part):
    shifts = jax.random.randint(jax.random.fold_in(key, 13), (IFACE,), 0, NT).astype(jnp.int32)
    return shifts.at[0].set(NT // 2).astype(jnp.int32)


def place_ends(entries, key, least, high):
    index_at = [jax.random.randint(jax.random.fold_in(key, axis), (), 0, length) for axis, length in enumerate(entries.shape)]
    widest = entries.shape.index(max(entries.shape))
    next_to = index_at[:widest] + [(index_at[widest] + 1) % entries.shape[widest]] + index_at[widest + 1:]
    return entries.at[tuple(index_at)].set(least).at[tuple(next_to)].set(high)


def levels(own_key, dims, cuts, least, high):
    level = 1.0
    for position, parts in cuts:
        draws = jax.random.uniform(jax.random.fold_in(jax.random.fold_in(own_key, 6), position), (parts,), jnp.float32, least / len(cuts), high / len(cuts))
        level = level * jnp.repeat(jnp.exp(draws), dims[position] // parts).reshape((-1,) + (1,) * (len(dims) - 1 - position))
    return level


def normal_values(rng, shape, scale, most, cuts=(), kind=jnp.bfloat16):
    level = levels(rng, shape, cuts, -0.22, 0.18) if cuts else 1.0
    drawn = jax.random.normal(rng, shape, jnp.float32) * scale * level
    return jnp.minimum(jnp.maximum(drawn, -most), most).astype(kind)


def setup_inputs(seed: int = 0) -> dict:
    splits = jax.random.split(jax.random.key(seed), 13)
    state = normal_values(splits[0], (NT, NV, NB, BLOCK_CELLS), 1.0, 6.0, ((0, 16), (2, 32)), jnp.float32)
    right_side = normal_values(splits[1], (NT, NV, NB, BLOCK_CELLS), 1.0, 6.0, ((0, 16), (2, 32)), jnp.float32)
    couplings = jnp.clip(0.05 + 0.29999999 * jax.random.uniform(splits[2], (3, NT, NV, NB, BLOCK_CELLS), jnp.float32) ** levels(splits[2], (3, NT, NV, NB, BLOCK_CELLS), ((1, 16), (3, 32)), -0.2, 0.2), 0.05, 0.35)
    jac_corr = normal_values(splits[3], (NT, NV, NV, NB, BLOCK_CELLS), 0.06, 0.3, ((0, 16), (3, 32)), jnp.float32)
    spec_scale = jnp.clip(jnp.exp(math.log(0.05) - 2.3025851 * jax.random.uniform(splits[4], (NB, BLOCK_CELLS), jnp.float32) ** levels(splits[4], (NB, BLOCK_CELLS), ((0, 32),), -0.2, 0.2)), 0.005, 0.05)
    row_id = place_ends(jax.random.randint(splits[5], (NB,), 0, 3), jax.random.fold_in(splits[5], 1), 0, 2).astype(jnp.int32)
    send_index = place_ends(jax.random.randint(splits[6], (N_MESH * N_MESH, HALO_SLOTS), 0, BLK_DEV), jax.random.fold_in(splits[6], 1), 0, BLK_DEV - 1).astype(jnp.int32)
    recv_slot = draw_recv_slot(jax.random.fold_in(splits[12], 71), 0)
    iface_coef = jnp.clip(0.2 + 0.400000021 * jax.random.uniform(splits[8], (IFACE, BLOCK_CELLS), jnp.float32) ** levels(splits[8], (IFACE, BLOCK_CELLS), ((0, 32),), -0.2, 0.2), 0.2, 0.6)
    donor_index = draw_donor_index(jax.random.fold_in(splits[12], 71), 0)
    donor_weight = jnp.clip(0.2 + 0.8 * jax.random.uniform(splits[10], (IFACE, 2), jnp.float32) ** levels(splits[10], (IFACE, 2), ((0, 32),), -0.2, 0.2), 0.2, 1.0)
    phase_shift = draw_phase_shift(jax.random.fold_in(splits[12], 71), 0)
    return dict(state=state, right_side=right_side, couplings=couplings, jac_corr=jac_corr, spec_scale=spec_scale, row_id=row_id, send_index=send_index, recv_slot=recv_slot, iface_coef=iface_coef, donor_index=donor_index, donor_weight=donor_weight, phase_shift=phase_shift)


def spectral_table(length):
    row_ids = jnp.arange(length)[:, None]
    col_ids = jnp.arange(length)[None, :]
    offsets = row_ids - col_ids
    parity = 1.0 - 2.0 * (offsets % 2).astype(jnp.float32)
    angles = jnp.pi * offsets.astype(jnp.float32) / length
    on_diag = offsets == 0
    sine_safe = jnp.where(on_diag, 1.0, jnp.sin(angles))
    first = jnp.where(on_diag, 0.0, 0.5 * parity * jnp.cos(angles) / sine_safe)
    diag_value = -(length * length + 2.0) / 12.0
    second = jnp.where(on_diag, diag_value, -0.5 * parity / (sine_safe * sine_safe))
    return first - 0.1 * second


def line_terms(field, couplings):
    zeros_col = jnp.zeros_like(field[..., :1])
    below = jnp.concatenate([zeros_col, field[..., :-1]], axis=-1)
    above = jnp.concatenate([field[..., 1:], zeros_col], axis=-1)
    return couplings[0] * below + couplings[1] * above


def jacobi_update(total_rhs, jac_corr):
    updated = 0.35 * total_rhs + jnp.einsum("nvwbc,nwbc->nvbc", jac_corr, total_rhs, precision=lax.Precision.HIGHEST)
    return updated.at[:, -1].set(jnp.maximum(updated[:, -1], 0.0))


def donor_mix(donor_pool, donor_index, donor_weight):
    first_part = donor_pool[:, :, donor_index[:, 0]] * donor_weight[:, 0][:, None]
    second_part = donor_pool[:, :, donor_index[:, 1]] * donor_weight[:, 1][:, None]
    return first_part + second_part


def phase_pick(combined, shift_src):
    targets = jnp.arange(combined.shape[2])[None, :]
    picked = combined[shift_src, :, targets]
    return jnp.transpose(picked, (0, 2, 1, 3))


def reference(state, right_side, couplings, jac_corr, spec_scale, row_id, send_index, recv_slot, iface_coef, donor_index, donor_weight, phase_shift):
    table = spectral_table(NT)
    owner = jnp.arange(NB) // BLK_DEV
    source_dev = recv_slot // HALO_SLOTS
    halo_block = source_dev * BLK_DEV + send_index[source_dev * N_MESH + owner, recv_slot % HALO_SLOTS]
    row_factor = 1.0 + 0.5 * row_id.astype(jnp.float32)
    frequency = spec_scale * row_factor[:, None]
    shift_src = (jnp.arange(NT)[:, None] + phase_shift[None, :]) % NT
    field = state
    for sweep_index in range(SWEEPS):
        spectral = jnp.einsum("nm,mvbc->nvbc", table, field, precision=lax.Precision.HIGHEST)
        halo_vals = field[:, :, halo_block]
        faces = field.reshape(NT, NV, N_MESH, BLK_DEV, BLOCK_CELLS)[:, :, :, :IF_DEV].reshape(NT, NV, IFACE, BLOCK_CELLS)
        combined = donor_mix(faces, donor_index, donor_weight)
        iface_term = iface_coef * phase_pick(combined, shift_src)
        total_rhs = right_side + line_terms(field, couplings) + couplings[2] * halo_vals - frequency * spectral
        total_rhs = total_rhs.reshape(NT, NV, N_MESH, BLK_DEV, BLOCK_CELLS)
        total_rhs = total_rhs.at[:, :, :, :IF_DEV].add(iface_term.reshape(NT, NV, N_MESH, IF_DEV, BLOCK_CELLS))
        total_rhs = total_rhs.reshape(NT, NV, NB, BLOCK_CELLS)
        field = jacobi_update(total_rhs, jac_corr)
    return field
```

```python
import jax
import jax.numpy as jnp
import numpy as np
from jax import lax
from jax.experimental import pallas as pl
from jax.experimental.pallas import tpu as pltpu
from jax.sharding import PartitionSpec as P

NT = 16
NV = 6
CELLS = 128
BLK = 64
NMESH = 32
ROWS = NV * BLK
PIECE = ROWS // NT
SLOT = 4 * NV
BACK = PIECE + 16
SWEEPS = 2
F32 = jnp.float32


def circulant_row():
    k = np.arange(NT, dtype=np.float64)
    parity = 1.0 - 2.0 * (k % 2)
    angle = np.pi * k / NT
    sine = np.where(k == 0, 1.0, np.sin(angle))
    first = np.where(k == 0, 0.0, 0.5 * parity * np.cos(angle) / sine)
    second = np.where(k == 0, -(NT * NT + 2.0) / 12.0, -0.5 * parity / (sine * sine))
    return [float(v) for v in (first - 0.1 * second)]


TABLE = circulant_row()


def pack_blocks(field, send, out):
    faces = [field[pl.ds(b, NV, stride=BLK), :] for b in range(2)]
    for dst in range(NMESH):
        for s in range(2):
            blk = send[s, dst]
            out[pl.ds(dst * SLOT + s * NV, NV), :] = field[pl.ds(blk, NV, stride=BLK), :]
        for b in range(2):
            out[pl.ds(dst * SLOT + (2 + b) * NV, NV), :] = faces[b]


def pack_kernel(field, send, out):
    pack_blocks(field, send, out)


def spectral_kernel(pieces, blocks, donor, weight, out):
    for t in range(PIECE // 8):
        rows = [pieces[pl.ds(m * PIECE + t * 8, 8), :] for m in range(NT)]
        for n in range(NT):
            acc = rows[0] * TABLE[n % NT]
            for m in range(1, NT):
                acc = acc + rows[m] * TABLE[(n - m) % NT]
            out[pl.ds(n * BACK + t * 8, 8), :] = acc
    for j in range(2):
        total = None
        for k in range(2):
            who = donor[j, k]
            row = (who // 2) * SLOT + (2 + who % 2) * NV
            part = blocks[pl.ds(row, NV), :] * weight[j, k]
            total = part if total is None else total + part
        for n in range(NT):
            out[pl.ds(n * BACK + PIECE + j * 8, NV), :] = total


def update_kernel(last, field, right, coup, jac, spec, row_id, recv, coef, shift, inst, blocks, back, *rest):
    if last:
        out, halo, freq = rest
    else:
        send, out, packed, halo, freq = rest
    for b in range(BLK):
        slot = recv[b]
        row = (slot // 2) * SLOT + (slot % 2) * NV
        halo[pl.ds(b, NV, stride=BLK), :] = blocks[pl.ds(row, NV), :]
        freq[pl.ds(b, 1), :] = spec[pl.ds(b, 1), :] * (1.0 + 0.5 * row_id[b].astype(F32))
    lane = lax.broadcasted_iota(jnp.int32, (8, CELLS), 1)
    sub = lax.broadcasted_iota(jnp.int32, (8, CELLS), 0)
    not_first = lane > 0
    not_last = lane < CELLS - 1
    mix_rows = [((inst[0] + shift[j]) % NT) * BACK + PIECE + j * 8 for j in range(2)]
    for t in range(BLK // 8):
        total = []
        f = freq[pl.ds(t * 8, 8), :]
        for v in range(NV):
            r = v * BLK + t * 8
            here = field[pl.ds(r, 8), :]
            below = jnp.where(not_first, pltpu.roll(here, 1, 1), 0.0)
            above = jnp.where(not_last, pltpu.roll(here, CELLS - 1, 1), 0.0)
            p, q = r // PIECE, r % PIECE
            val = right[pl.ds(r, 8), :]
            val = val + (coup[pl.ds(r, 8), :] * below + coup[pl.ds(ROWS + r, 8), :] * above)
            val = val + coup[pl.ds(2 * ROWS + r, 8), :] * halo[pl.ds(r, 8), :]
            val = val - f * back[pl.ds(p * BACK + q, 8), :]
            if t == 0:
                for j in range(2):
                    mix = coef[pl.ds(j, 1), :] * back[pl.ds(mix_rows[j] + v, 1), :]
                    val = jnp.where(sub == j, val + mix, val)
            total.append(val)
        for v in range(NV):
            new = 0.35 * total[v]
            for w in range(NV):
                new = new + jac[pl.ds((v * NV + w) * BLK + t * 8, 8), :] * total[w]
            if v == NV - 1:
                new = jnp.maximum(new, 0.0)
            out[pl.ds(v * BLK + t * 8, 8), :] = new
    if not last:
        pack_blocks(out, send, packed)


def vmem():
    return pl.BlockSpec(memory_space=pltpu.VMEM)


def smem():
    return pl.BlockSpec(memory_space=pltpu.SMEM)


def rows_of(n):
    return jax.ShapeDtypeStruct((n, CELLS), F32)


def swap(x, axis, parts):
    rows = x.shape[0]
    y = lax.all_to_all(x.reshape(parts, rows // parts, CELLS), axis, 0, 0, tiled=True)
    return y.reshape(rows, CELLS)


def per_device(
    state,
    right_side,
    couplings,
    jac_corr,
    spec_scale,
    row_id,
    send_index,
    recv_slot,
    iface_coef,
    donor_index,
    donor_weight,
    phase_shift,
):
    field = state.reshape(ROWS, CELLS)
    right = right_side.reshape(ROWS, CELLS)
    coup = couplings.reshape(3 * ROWS, CELLS)
    jac = jac_corr.reshape(NV * ROWS, CELLS)
    send = send_index.T
    inst = lax.axis_index("inst").astype(jnp.int32).reshape(1)

    packed = pl.pallas_call(
        pack_kernel,
        out_shape=rows_of(NMESH * SLOT),
        in_specs=[vmem(), smem()],
        out_specs=vmem(),
        name="pack",
    )(field, send)
    for sweep in range(SWEEPS):
        last = sweep == SWEEPS - 1
        with jax.named_scope("ahead"):
            pieces = swap(field, "inst", NT)
        with jax.named_scope("blocks"):
            blocks = swap(packed, "mesh", NMESH)
        back = pl.pallas_call(
            spectral_kernel,
            out_shape=rows_of(NT * BACK),
            in_specs=[vmem(), vmem(), smem(), smem()],
            out_specs=vmem(),
            name="spectral",
        )(pieces, blocks, donor_index, donor_weight)
        with jax.named_scope("back"):
            back = swap(back, "inst", NT)
        ins = [field, right, coup, jac, spec_scale, row_id, recv_slot, iface_coef, phase_shift, inst, blocks, back]
        specs = [vmem(), vmem(), vmem(), vmem(), vmem(), smem(), smem(), vmem(), smem(), smem(), vmem(), vmem()]
        shapes = [rows_of(ROWS)]
        if not last:
            ins.append(send)
            specs.append(smem())
            shapes.append(rows_of(NMESH * SLOT))
        res = pl.pallas_call(
            lambda *refs, last=last: update_kernel(last, *refs),
            out_shape=shapes,
            in_specs=specs,
            out_specs=[vmem()] * len(shapes),
            scratch_shapes=[pltpu.VMEM((ROWS, CELLS), F32), pltpu.VMEM((BLK, CELLS), F32)],
            name="update",
        )(*ins)
        field = res[0]
        if not last:
            packed = res[1]
    return field.reshape(1, NV, BLK, CELLS)


def solution(mesh):
    return jax.shard_map(
        per_device,
        mesh=mesh,
        in_specs=(
            P("inst", None, "mesh", None),
            P("inst", None, "mesh", None),
            P(None, "inst", None, "mesh", None),
            P("inst", None, None, "mesh", None),
            P("mesh", None),
            P("mesh"),
            P("mesh", None),
            P("mesh"),
            P("mesh", None),
            P("mesh", None),
            P("mesh", None),
            P("mesh"),
        ),
        out_specs=P("inst", None, "mesh", None),
        check_vma=False,
    )
```

```python
import jax
import jax.numpy as jnp
import numpy as np
from jax import lax
from jax.experimental import pallas as pl
from jax.experimental.pallas import tpu as pltpu
from jax.sharding import PartitionSpec as P

NT = 16
NV = 6
CELLS = 128
BLK = 64
NMESH = 32
ROWS = NV * BLK
PIECE = ROWS // NT
SLOT = 4 * NV
LEG = PIECE + 1
SWEEPS = 2
F32 = jnp.float32


def circulant_row():
    k = np.arange(NT, dtype=np.float64)
    parity = 1.0 - 2.0 * (k % 2)
    angle = np.pi * k / NT
    sine = np.where(k == 0, 1.0, np.sin(angle))
    first = np.where(k == 0, 0.0, 0.5 * parity * np.cos(angle) / sine)
    second = np.where(k == 0, -(NT * NT + 2.0) / 12.0, -0.5 * parity / (sine * sine))
    return [float(v) for v in (first - 0.1 * second)]


TABLE = circulant_row()


def pack_blocks(field, send, out):
    faces = [field[pl.ds(b, NV, stride=BLK), :] for b in range(2)]
    for dst in range(NMESH):
        for s in range(2):
            blk = send[s, dst]
            out[pl.ds(dst * SLOT + s * NV, NV), :] = field[pl.ds(blk, NV, stride=BLK), :]
        for b in range(2):
            out[pl.ds(dst * SLOT + (2 + b) * NV, NV), :] = faces[b]


def pack_kernel(field, send, out):
    pack_blocks(field, send, out)


def mix_kernel(field, blocks, donor, weight, out):
    for p in range(NT):
        out[pl.ds(p * LEG, PIECE), :] = field[pl.ds(p * PIECE, PIECE), :]
    for j in range(2):
        total = None
        for k in range(2):
            who = donor[j, k]
            row = (who // 2) * SLOT + (2 + who % 2) * NV
            part = blocks[pl.ds(row, NV), :] * weight[j, k]
            total = part if total is None else total + part
        for v in range(NV):
            out[pl.ds((j * NV + v) * LEG + PIECE, 1), :] = total[v : v + 1]
    for p in range(2 * NV, NT):
        out[pl.ds(p * LEG + PIECE, 1), :] = jnp.zeros((1, CELLS), F32)


def spectral_kernel(legs, shift, inst, out):
    for t in range(PIECE // 8):
        rows = [legs[pl.ds(m * LEG + t * 8, 8), :] for m in range(NT)]
        for n in range(NT):
            acc = rows[0] * TABLE[n % NT]
            for m in range(1, NT):
                acc = acc + rows[m] * TABLE[(n - m) % NT]
            out[pl.ds(n * LEG + t * 8, 8), :] = acc
    turn = jnp.where(inst[0] < NV, shift[0], shift[1])
    for n in range(NT):
        src = ((n + turn) % NT) * LEG + PIECE
        out[pl.ds(n * LEG + PIECE, 1), :] = legs[pl.ds(src, 1), :]


def update_kernel(last, field, right, coup, jac, spec, row_id, recv, coef, blocks, back, *rest):
    if last:
        out, halo, freq = rest
    else:
        send, out, packed, halo, freq = rest
    for b in range(BLK):
        slot = recv[b]
        row = (slot // 2) * SLOT + (slot % 2) * NV
        halo[pl.ds(b, NV, stride=BLK), :] = blocks[pl.ds(row, NV), :]
        freq[pl.ds(b, 1), :] = spec[pl.ds(b, 1), :] * (1.0 + 0.5 * row_id[b].astype(F32))
    lane = lax.broadcasted_iota(jnp.int32, (8, CELLS), 1)
    sub = lax.broadcasted_iota(jnp.int32, (8, CELLS), 0)
    not_first = lane > 0
    not_last = lane < CELLS - 1
    for t in range(BLK // 8):
        total = []
        f = freq[pl.ds(t * 8, 8), :]
        for v in range(NV):
            r = v * BLK + t * 8
            here = field[pl.ds(r, 8), :]
            below = jnp.where(not_first, pltpu.roll(here, 1, 1), 0.0)
            above = jnp.where(not_last, pltpu.roll(here, CELLS - 1, 1), 0.0)
            p, q = r // PIECE, r % PIECE
            val = right[pl.ds(r, 8), :]
            val = val + (coup[pl.ds(r, 8), :] * below + coup[pl.ds(ROWS + r, 8), :] * above)
            val = val + coup[pl.ds(2 * ROWS + r, 8), :] * halo[pl.ds(r, 8), :]
            val = val - f * back[pl.ds(p * LEG + q, 8), :]
            if t == 0:
                for j in range(2):
                    mix = coef[pl.ds(j, 1), :] * back[pl.ds((j * NV + v) * LEG + PIECE, 1), :]
                    val = jnp.where(sub == j, val + mix, val)
            total.append(val)
        for v in range(NV):
            new = 0.35 * total[v]
            for w in range(NV):
                new = new + jac[pl.ds((v * NV + w) * BLK + t * 8, 8), :] * total[w]
            if v == NV - 1:
                new = jnp.maximum(new, 0.0)
            out[pl.ds(v * BLK + t * 8, 8), :] = new
    if not last:
        pack_blocks(out, send, packed)


def vmem():
    return pl.BlockSpec(memory_space=pltpu.VMEM)


def smem():
    return pl.BlockSpec(memory_space=pltpu.SMEM)


def rows_of(n):
    return jax.ShapeDtypeStruct((n, CELLS), F32)


def swap(x, axis, parts):
    rows = x.shape[0]
    y = lax.all_to_all(x.reshape(parts, rows // parts, CELLS), axis, 0, 0, tiled=True)
    return y.reshape(rows, CELLS)


def swap_rows(x):
    y = lax.all_to_all(x.reshape(NT, LEG, 1, CELLS), "inst", 0, 0, tiled=True)
    return y.reshape(NT * LEG, CELLS)


def per_device(
    state,
    right_side,
    couplings,
    jac_corr,
    spec_scale,
    row_id,
    send_index,
    recv_slot,
    iface_coef,
    donor_index,
    donor_weight,
    phase_shift,
):
    field = state.reshape(ROWS, CELLS)
    right = right_side.reshape(ROWS, CELLS)
    coup = couplings.reshape(3 * ROWS, CELLS)
    jac = jac_corr.reshape(NV * ROWS, CELLS)
    send = send_index.T
    inst = lax.axis_index("inst").astype(jnp.int32).reshape(1)

    packed = pl.pallas_call(
        pack_kernel,
        out_shape=rows_of(NMESH * SLOT),
        in_specs=[vmem(), smem()],
        out_specs=vmem(),
        name="pack",
    )(field, send)
    for sweep in range(SWEEPS):
        last = sweep == SWEEPS - 1
        blocks = swap(packed, "mesh", NMESH)
        legs = pl.pallas_call(
            mix_kernel,
            out_shape=rows_of(NT * LEG),
            in_specs=[vmem(), vmem(), smem(), smem()],
            out_specs=vmem(),
            name="mix",
        )(field, blocks, donor_index, donor_weight)
        legs = swap_rows(legs)
        back = pl.pallas_call(
            spectral_kernel,
            out_shape=rows_of(NT * LEG),
            in_specs=[vmem(), smem(), smem()],
            out_specs=vmem(),
            name="spectral",
        )(legs, phase_shift, inst)
        back = swap_rows(back)
        ins = [field, right, coup, jac, spec_scale, row_id, recv_slot, iface_coef, blocks, back]
        specs = [vmem(), vmem(), vmem(), vmem(), vmem(), smem(), smem(), vmem(), vmem(), vmem()]
        shapes = [rows_of(ROWS)]
        if not last:
            ins.append(send)
            specs.append(smem())
            shapes.append(rows_of(NMESH * SLOT))
        res = pl.pallas_call(
            lambda *refs, last=last: update_kernel(last, *refs),
            out_shape=shapes,
            in_specs=specs,
            out_specs=[vmem()] * len(shapes),
            scratch_shapes=[pltpu.VMEM((ROWS, CELLS), F32), pltpu.VMEM((BLK, CELLS), F32)],
            name="update",
        )(*ins)
        field = res[0]
        if not last:
            packed = res[1]
    return field.reshape(1, NV, BLK, CELLS)


def solution(mesh):
    return jax.shard_map(
        per_device,
        mesh=mesh,
        in_specs=(
            P("inst", None, "mesh", None),
            P("inst", None, "mesh", None),
            P(None, "inst", None, "mesh", None),
            P("inst", None, None, "mesh", None),
            P("mesh", None),
            P("mesh"),
            P("mesh", None),
            P("mesh"),
            P("mesh", None),
            P("mesh", None),
            P("mesh", None),
            P("mesh"),
        ),
        out_specs=P("inst", None, "mesh", None),
        check_vma=False,
    )
```

```python
import jax
import jax.numpy as jnp
import numpy as np
from jax import lax
from jax.experimental import pallas as pl
from jax.experimental.pallas import tpu as pltpu
from jax.sharding import PartitionSpec as P

NT = 16
NV = 6
CELLS = 128
BLK = 64
NMESH = 32
ROWS = NV * BLK
PIECE = ROWS // NT
SLOT = 4 * NV
LEG = PIECE + 1
SWEEPS = 2
F32 = jnp.float32


def circulant_row():
    k = np.arange(NT, dtype=np.float64)
    parity = 1.0 - 2.0 * (k % 2)
    angle = np.pi * k / NT
    sine = np.where(k == 0, 1.0, np.sin(angle))
    first = np.where(k == 0, 0.0, 0.5 * parity * np.cos(angle) / sine)
    second = np.where(k == 0, -(NT * NT + 2.0) / 12.0, -0.5 * parity / (sine * sine))
    return [float(v) for v in (first - 0.1 * second)]


TABLE = circulant_row()


def pack_blocks(field, send, out):
    faces = [field[pl.ds(b, NV, stride=BLK), :] for b in range(2)]
    for dst in range(NMESH):
        for s in range(2):
            blk = send[s, dst]
            out[pl.ds(dst * SLOT + s * NV, NV), :] = field[pl.ds(blk, NV, stride=BLK), :]
        for b in range(2):
            out[pl.ds(dst * SLOT + (2 + b) * NV, NV), :] = faces[b]


def pack_kernel(field, send, out, legs):
    pack_blocks(field, send, out)
    for p in range(NT):
        legs[pl.ds(p * LEG, PIECE), :] = field[pl.ds(p * PIECE, PIECE), :]
        legs[pl.ds(p * LEG + PIECE, 1), :] = jnp.zeros((1, CELLS), F32)


def mix_kernel(legs, blocks, donor, weight, out):
    out[...] = legs[...]
    for j in range(2):
        total = None
        for k in range(2):
            who = donor[j, k]
            row = (who // 2) * SLOT + (2 + who % 2) * NV
            part = blocks[pl.ds(row, NV), :] * weight[j, k]
            total = part if total is None else total + part
        for v in range(NV):
            out[pl.ds((j * NV + v) * LEG + PIECE, 1), :] = total[v : v + 1]


def spectral_kernel(legs, shift, inst, out):
    for t in range(PIECE // 8):
        rows = [legs[pl.ds(m * LEG + t * 8, 8), :] for m in range(NT)]
        for n in range(NT):
            acc = rows[0] * TABLE[n % NT]
            for m in range(1, NT):
                acc = acc + rows[m] * TABLE[(n - m) % NT]
            out[pl.ds(n * LEG + t * 8, 8), :] = acc
    turn = jnp.where(inst[0] < NV, shift[0], shift[1])
    mixes = legs[pl.ds(PIECE, NT, stride=LEG), :]
    out[pl.ds(PIECE, NT, stride=LEG), :] = pltpu.roll(mixes, NT - turn, 0)


def update_kernel(last, field, right, coup, jac, spec, row_id, recv, coef, blocks, back, *rest):
    if last:
        out, halo, freq = rest
    else:
        send, out, packed, legs, halo, freq = rest
    for b in range(BLK):
        slot = recv[b]
        row = (slot // 2) * SLOT + (slot % 2) * NV
        halo[pl.ds(b, NV, stride=BLK), :] = blocks[pl.ds(row, NV), :]
        freq[pl.ds(b, 1), :] = spec[pl.ds(b, 1), :] * (1.0 + 0.5 * row_id[b].astype(F32))
    lane = lax.broadcasted_iota(jnp.int32, (8, CELLS), 1)
    sub = lax.broadcasted_iota(jnp.int32, (8, CELLS), 0)
    not_first = lane > 0
    not_last = lane < CELLS - 1
    for t in range(BLK // 8):
        total = []
        f = freq[pl.ds(t * 8, 8), :]
        for v in range(NV):
            r = v * BLK + t * 8
            here = field[pl.ds(r, 8), :]
            below = jnp.where(not_first, pltpu.roll(here, 1, 1), 0.0)
            above = jnp.where(not_last, pltpu.roll(here, CELLS - 1, 1), 0.0)
            p, q = r // PIECE, r % PIECE
            val = right[pl.ds(r, 8), :]
            val = val + (coup[pl.ds(r, 8), :] * below + coup[pl.ds(ROWS + r, 8), :] * above)
            val = val + coup[pl.ds(2 * ROWS + r, 8), :] * halo[pl.ds(r, 8), :]
            val = val - f * back[pl.ds(p * LEG + q, 8), :]
            if t == 0:
                for j in range(2):
                    mix = coef[pl.ds(j, 1), :] * back[pl.ds((j * NV + v) * LEG + PIECE, 1), :]
                    val = jnp.where(sub == j, val + mix, val)
            total.append(val)
        for v in range(NV):
            new = 0.35 * total[v]
            for w in range(NV):
                new = new + jac[pl.ds((v * NV + w) * BLK + t * 8, 8), :] * total[w]
            if v == NV - 1:
                new = jnp.maximum(new, 0.0)
            r = v * BLK + t * 8
            out[pl.ds(r, 8), :] = new
            if not last:
                legs[pl.ds((r // PIECE) * LEG + r % PIECE, 8), :] = new
    if not last:
        pack_blocks(out, send, packed)


def vmem():
    return pl.BlockSpec(memory_space=pltpu.VMEM)


def smem():
    return pl.BlockSpec(memory_space=pltpu.SMEM)


def rows_of(n):
    return jax.ShapeDtypeStruct((n, CELLS), F32)


def swap(x, axis, parts):
    rows = x.shape[0]
    y = lax.all_to_all(x.reshape(parts, rows // parts, CELLS), axis, 0, 0, tiled=True)
    return y.reshape(rows, CELLS)


def swap_rows(x):
    y = lax.all_to_all(x.reshape(NT, LEG, 1, CELLS), "inst", 0, 0, tiled=True)
    return y.reshape(NT * LEG, CELLS)


def per_device(
    state,
    right_side,
    couplings,
    jac_corr,
    spec_scale,
    row_id,
    send_index,
    recv_slot,
    iface_coef,
    donor_index,
    donor_weight,
    phase_shift,
):
    near = lambda x: pltpu.with_memory_space_constraint(x, pltpu.VMEM)
    small = lambda x: x
    field = state.reshape(ROWS, CELLS)
    right = near(right_side.reshape(ROWS, CELLS))
    coup = near(couplings.reshape(3 * ROWS, CELLS))
    jac = near(jac_corr.reshape(NV * ROWS, CELLS))
    spec = near(spec_scale)
    send = small(send_index.T)
    inst = small(lax.axis_index("inst").astype(jnp.int32).reshape(1))
    donor = small(donor_index)
    weight = small(donor_weight)
    shift = small(phase_shift)
    recv = small(recv_slot)
    blade = small(row_id)

    packed, legs = pl.pallas_call(
        pack_kernel,
        out_shape=[rows_of(NMESH * SLOT), rows_of(NT * LEG)],
        in_specs=[vmem(), smem()],
        out_specs=[vmem()] * 2,
        name="pack",
        compiler_params=pltpu.CompilerParams(vmem_limit_bytes=8 << 20),
    )(near(field), send)
    for sweep in range(SWEEPS):
        last = sweep == SWEEPS - 1
        blocks = near(swap(packed, "mesh", NMESH))
        legs = pl.pallas_call(
            mix_kernel,
            out_shape=rows_of(NT * LEG),
            in_specs=[vmem(), vmem(), smem(), smem()],
            out_specs=vmem(),
            input_output_aliases={0: 0},
            name="mix",
            compiler_params=pltpu.CompilerParams(vmem_limit_bytes=8 << 20),
        )(near(legs), blocks, donor, weight)
        legs = near(swap_rows(legs))
        back = pl.pallas_call(
            spectral_kernel,
            out_shape=rows_of(NT * LEG),
            in_specs=[vmem(), smem(), smem()],
            out_specs=vmem(),
            input_output_aliases={0: 0},
            name="spectral",
            compiler_params=pltpu.CompilerParams(vmem_limit_bytes=8 << 20),
        )(legs, shift, inst)
        back = near(swap_rows(back))
        ins = [near(field), right, coup, jac, spec, blade, recv, iface_coef, blocks, back]
        specs = [vmem(), vmem(), vmem(), vmem(), vmem(), smem(), smem(), vmem(), vmem(), vmem()]
        shapes = [rows_of(ROWS)]
        alias = {}
        if not last:
            ins.append(send)
            specs.append(smem())
            shapes += [rows_of(NMESH * SLOT), rows_of(NT * LEG)]
            alias = {0: 0, 8: 1, 9: 2}
        res = pl.pallas_call(
            lambda *refs, last=last: update_kernel(last, *refs),
            out_shape=shapes,
            in_specs=specs,
            out_specs=[vmem()] * len(shapes),
            scratch_shapes=[pltpu.VMEM((ROWS, CELLS), F32), pltpu.VMEM((BLK, CELLS), F32)],
            input_output_aliases=alias,
            name="update",
            compiler_params=pltpu.CompilerParams(vmem_limit_bytes=8 << 20),
        )(*ins)
        field = res[0]
        if not last:
            packed, legs = res[1], res[2]
    return field.reshape(1, NV, BLK, CELLS)


def solution(mesh):
    return jax.shard_map(
        per_device,
        mesh=mesh,
        in_specs=(
            P("inst", None, "mesh", None),
            P("inst", None, "mesh", None),
            P(None, "inst", None, "mesh", None),
            P("inst", None, None, "mesh", None),
            P("mesh", None),
            P("mesh"),
            P("mesh", None),
            P("mesh"),
            P("mesh", None),
            P("mesh", None),
            P("mesh", None),
            P("mesh"),
        ),
        out_specs=P("inst", None, "mesh", None),
        check_vma=False,
    )
```

```python
import jax
import jax.numpy as jnp
import numpy as np
from jax import lax
from jax.experimental import pallas as pl
from jax.experimental.pallas import tpu as pltpu
from jax.sharding import PartitionSpec as P

NT = 16
NV = 6
CELLS = 128
BLK = 64
NMESH = 32
ROWS = NV * BLK
PIECE = ROWS // NT
SLOT = 4 * NV
LEG = PIECE + 1
SWEEPS = 2
STALL = (700, 700)
F32 = jnp.float32


def circulant_row():
    k = np.arange(NT, dtype=np.float64)
    parity = 1.0 - 2.0 * (k % 2)
    angle = np.pi * k / NT
    sine = np.where(k == 0, 1.0, np.sin(angle))
    first = np.where(k == 0, 0.0, 0.5 * parity * np.cos(angle) / sine)
    second = np.where(k == 0, -(NT * NT + 2.0) / 12.0, -0.5 * parity / (sine * sine))
    return [float(v) for v in (first - 0.1 * second)]


TABLE = circulant_row()
EVEN = [0.5 * (TABLE[k] + TABLE[(k + NT // 2) % NT]) for k in range(NT)]
ODD = [0.5 * (TABLE[k] - TABLE[(k + NT // 2) % NT]) for k in range(NT)]


def pack_blocks(field, send, out):
    faces = [field[pl.ds(b, NV, stride=BLK), :] for b in range(2)]
    for dst in range(NMESH):
        for s in range(2):
            blk = send[s, dst]
            out[pl.ds(dst * SLOT + s * NV, NV), :] = field[pl.ds(blk, NV, stride=BLK), :]
        for b in range(2):
            out[pl.ds(dst * SLOT + (2 + b) * NV, NV), :] = faces[b]


def pack_kernel(field, send, out):
    pack_blocks(field, send, out)


def mix_kernel(stall, legs, field, blocks, donor, weight, place, out, spin):
    for p in range(NT):
        out[pl.ds(p * LEG, PIECE), :] = field[pl.ds(p * PIECE, PIECE), :]
    for p in range(2 * NV, NT):
        out[pl.ds(p * LEG + PIECE, 1), :] = jnp.zeros((1, CELLS), F32)
    for j in range(2):
        total = None
        for k in range(2):
            who = donor[j, k]
            row = (who // 2) * SLOT + (2 + who % 2) * NV
            part = blocks[pl.ds(row, NV), :] * weight[j, k]
            total = part if total is None else total + part
        for v in range(NV):
            out[pl.ds((j * NV + v) * LEG + PIECE, 1), :] = total[v : v + 1]
    turns = jnp.where(place[1] % 2 == 0, stall, 0)
    spin[...] = lax.fori_loop(0, turns, lambda i, x: pltpu.roll(x, 1, 1), field[pl.ds(0, 8), :])


def spectral_kernel(legs, shift, inst, out):
    half = NT // 2
    for t in range(PIECE // 8):
        rows = [legs[pl.ds(m * LEG + t * 8, 8), :] for m in range(NT)]
        plus = [rows[m] + rows[m + half] for m in range(half)]
        minus = [rows[m] - rows[m + half] for m in range(half)]
        for n in range(half):
            a = plus[0] * EVEN[n]
            b = minus[0] * ODD[n]
            for m in range(1, half):
                a = a + plus[m] * EVEN[(n - m) % NT]
                b = b + minus[m] * ODD[(n - m) % NT]
            out[pl.ds(n * LEG + t * 8, 8), :] = a + b
            out[pl.ds((n + half) * LEG + t * 8, 8), :] = a - b
    turn = jnp.where(inst[0] < NV, shift[0], shift[1])
    mixes = legs[pl.ds(PIECE, NT, stride=LEG), :]
    out[pl.ds(PIECE, NT, stride=LEG), :] = pltpu.roll(mixes, NT - turn, 0)


def update_kernel(last, field, right, coup, jac, spec, row_id, recv, coef, blocks, back, *rest):
    if last:
        out, halo, freq = rest
    else:
        send, fresh, out, packed, halo, freq = rest
    for b in range(BLK):
        slot = recv[b]
        row = (slot // 2) * SLOT + (slot % 2) * NV
        halo[pl.ds(b, NV, stride=BLK), :] = blocks[pl.ds(row, NV), :]
        freq[pl.ds(b, 1), :] = spec[pl.ds(b, 1), :] * (1.0 + 0.5 * row_id[b].astype(F32))
    lane = lax.broadcasted_iota(jnp.int32, (8, CELLS), 1)
    sub = lax.broadcasted_iota(jnp.int32, (8, CELLS), 0)
    not_first = lane > 0
    not_last = lane < CELLS - 1
    for t in range(BLK // 8):
        total = []
        f = freq[pl.ds(t * 8, 8), :]
        for v in range(NV):
            r = v * BLK + t * 8
            here = field[pl.ds(r, 8), :]
            below = jnp.where(not_first, pltpu.roll(here, 1, 1), 0.0)
            above = jnp.where(not_last, pltpu.roll(here, CELLS - 1, 1), 0.0)
            p, q = r // PIECE, r % PIECE
            val = right[pl.ds(r, 8), :]
            val = val + (coup[pl.ds(r, 8), :] * below + coup[pl.ds(ROWS + r, 8), :] * above)
            val = val + coup[pl.ds(2 * ROWS + r, 8), :] * halo[pl.ds(r, 8), :]
            val = val - f * back[pl.ds(p * LEG + q, 8), :]
            if t == 0:
                for j in range(2):
                    mix = coef[pl.ds(j, 1), :] * back[pl.ds((j * NV + v) * LEG + PIECE, 1), :]
                    val = jnp.where(sub == j, val + mix, val)
            total.append(val)
        for v in range(NV):
            new = 0.35 * total[v]
            for w in range(NV):
                new = new + jac[pl.ds((v * NV + w) * BLK + t * 8, 8), :] * total[w]
            if v == NV - 1:
                new = jnp.maximum(new, 0.0)
            out[pl.ds(v * BLK + t * 8, 8), :] = new
    if not last:
        pack_blocks(out, send, packed)


def vmem():
    return pl.BlockSpec(memory_space=pltpu.VMEM)


def smem():
    return pl.BlockSpec(memory_space=pltpu.SMEM)


def rows_of(n):
    return jax.ShapeDtypeStruct((n, CELLS), F32)


def swap(x, axis, parts):
    rows = x.shape[0]
    y = lax.all_to_all(x.reshape(parts, rows // parts, CELLS), axis, 0, 0, tiled=True)
    return y.reshape(rows, CELLS)


def swap_rows(x):
    y = lax.all_to_all(x.reshape(NT, LEG, 1, CELLS), "inst", 0, 0, tiled=True)
    return y.reshape(NT * LEG, CELLS)


def per_device(
    state,
    right_side,
    couplings,
    jac_corr,
    spec_scale,
    row_id,
    send_index,
    recv_slot,
    iface_coef,
    donor_index,
    donor_weight,
    phase_shift,
):
    near = lambda x: pltpu.with_memory_space_constraint(x, pltpu.VMEM)
    far = lambda x: pltpu.with_memory_space_constraint(x, pltpu.HBM)
    field = state.reshape(ROWS, CELLS)
    right = near(right_side.reshape(ROWS, CELLS))
    coup = near(couplings.reshape(3 * ROWS, CELLS))
    jac = near(jac_corr.reshape(NV * ROWS, CELLS))
    spec = near(spec_scale)
    send = send_index.T
    place = jnp.stack([lax.axis_index("inst"), lax.axis_index("mesh")]).astype(jnp.int32)
    donor = donor_index
    weight = donor_weight
    shift = phase_shift
    recv = recv_slot
    blade = row_id

    packed = pl.pallas_call(
        pack_kernel,
        out_shape=rows_of(NMESH * SLOT),
        in_specs=[vmem(), smem()],
        out_specs=vmem(),
        name="pack",
        compiler_params=pltpu.CompilerParams(vmem_limit_bytes=8 << 20),
    )(far(field), far(send))
    fresh = jnp.zeros((ROWS, CELLS), F32)
    legs = jnp.zeros((NT * LEG, CELLS), F32)
    for sweep in range(SWEEPS):
        last = sweep == SWEEPS - 1
        blocks = near(swap(packed, "mesh", NMESH))
        legs = pl.pallas_call(
            lambda *refs, sweep=sweep: mix_kernel(STALL[sweep], *refs),
            out_shape=rows_of(NT * LEG),
            in_specs=[vmem(), vmem(), vmem(), smem(), smem(), smem()],
            out_specs=vmem(),
            scratch_shapes=[pltpu.VMEM((8, CELLS), F32)],
            input_output_aliases={0: 0},
            name="mix",
            compiler_params=pltpu.CompilerParams(vmem_limit_bytes=8 << 20),
        )(near(legs), near(field), blocks, donor, weight, place)
        legs = near(swap_rows(legs))
        back = pl.pallas_call(
            spectral_kernel,
            out_shape=rows_of(NT * LEG),
            in_specs=[vmem(), smem(), smem()],
            out_specs=vmem(),
            input_output_aliases={0: 0},
            name="spectral",
            compiler_params=pltpu.CompilerParams(vmem_limit_bytes=8 << 20),
        )(legs, shift, place)
        back = near(swap_rows(back))
        ins = [near(field), right, coup, jac, spec, blade, recv, iface_coef, blocks, back]
        specs = [vmem(), vmem(), vmem(), vmem(), vmem(), smem(), smem(), vmem(), vmem(), vmem()]
        shapes = [rows_of(ROWS)]
        alias = {}
        if not last:
            ins += [send, near(fresh)]
            specs += [smem(), vmem()]
            shapes.append(rows_of(NMESH * SLOT))
            alias = {11: 0, 8: 1}
        res = pl.pallas_call(
            lambda *refs, last=last: update_kernel(last, *refs),
            out_shape=shapes,
            in_specs=specs,
            out_specs=[vmem()] * len(shapes),
            scratch_shapes=[pltpu.VMEM((ROWS, CELLS), F32), pltpu.VMEM((BLK, CELLS), F32)],
            input_output_aliases=alias,
            name="update",
            compiler_params=pltpu.CompilerParams(vmem_limit_bytes=8 << 20),
        )(*ins)
        field = res[0]
        if not last:
            packed, legs = res[1], back
    return field.reshape(1, NV, BLK, CELLS)


def solution(mesh):
    return jax.shard_map(
        per_device,
        mesh=mesh,
        in_specs=(
            P("inst", None, "mesh", None),
            P("inst", None, "mesh", None),
            P(None, "inst", None, "mesh", None),
            P("inst", None, None, "mesh", None),
            P("mesh", None),
            P("mesh"),
            P("mesh", None),
            P("mesh"),
            P("mesh", None),
            P("mesh", None),
            P("mesh", None),
            P("mesh"),
        ),
        out_specs=P("inst", None, "mesh", None),
        check_vma=False,
    )
```

```python
import jax
import jax.numpy as jnp
import numpy as np
from jax import lax
from jax.experimental import pallas as pl
from jax.experimental.pallas import tpu as pltpu
from jax.sharding import PartitionSpec as P

NT = 16
NV = 6
CELLS = 128
BLK = 64
NMESH = 32
ROWS = NV * BLK
PIECE = ROWS // NT
SLOT = 4 * NV
LEG = PIECE + 1
SWEEPS = 2
STALL = (560, 560)
F32 = jnp.float32


def circulant_row():
    k = np.arange(NT, dtype=np.float64)
    parity = 1.0 - 2.0 * (k % 2)
    angle = np.pi * k / NT
    sine = np.where(k == 0, 1.0, np.sin(angle))
    first = np.where(k == 0, 0.0, 0.5 * parity * np.cos(angle) / sine)
    second = np.where(k == 0, -(NT * NT + 2.0) / 12.0, -0.5 * parity / (sine * sine))
    return [float(v) for v in (first - 0.1 * second)]


TABLE = circulant_row()
EVEN = [0.5 * (TABLE[k] + TABLE[(k + NT // 2) % NT]) for k in range(NT)]
ODD = [0.5 * (TABLE[k] - TABLE[(k + NT // 2) % NT]) for k in range(NT)]


def pack_blocks(field, send, out):
    faces = [field[pl.ds(b, NV, stride=BLK), :] for b in range(2)]
    for dst in range(NMESH):
        for s in range(2):
            blk = send[s, dst]
            out[pl.ds(dst * SLOT + s * NV, NV), :] = field[pl.ds(blk, NV, stride=BLK), :]
        for b in range(2):
            out[pl.ds(dst * SLOT + (2 + b) * NV, NV), :] = faces[b]


def pack_kernel(field, send, place, out_in, out):
    pack_blocks(field, send, out)


def local_terms(field, right, coup, spec, row_id, recv, blocks, part, freq, halo):
    for b in range(BLK):
        slot = recv[b]
        row = (slot // 2) * SLOT + (slot % 2) * NV
        halo[pl.ds(b, NV, stride=BLK), :] = blocks[pl.ds(row, NV), :]
        freq[pl.ds(b, 1), :] = spec[pl.ds(b, 1), :] * (1.0 + 0.5 * row_id[b].astype(F32))
    lane = lax.broadcasted_iota(jnp.int32, (8, CELLS), 1)
    not_first = lane > 0
    not_last = lane < CELLS - 1
    for t in range(ROWS // 8):
        r = t * 8
        here = field[pl.ds(r, 8), :]
        below = jnp.where(not_first, pltpu.roll(here, 1, 1), 0.0)
        above = jnp.where(not_last, pltpu.roll(here, CELLS - 1, 1), 0.0)
        val = right[pl.ds(r, 8), :]
        val = val + (coup[pl.ds(r, 8), :] * below + coup[pl.ds(ROWS + r, 8), :] * above)
        part[pl.ds(r, 8), :] = val + coup[pl.ds(2 * ROWS + r, 8), :] * halo[pl.ds(r, 8), :]


def mix_kernel(
    stall, legs, donor, weight, place, field, right, coup, spec, row_id, recv, blocks, part_in, freq_in,
    out, part, freq, halo, spin,
):
    for p in range(NT):
        out[pl.ds(p * LEG, PIECE), :] = field[pl.ds(p * PIECE, PIECE), :]
    for p in range(2 * NV, NT):
        out[pl.ds(p * LEG + PIECE, 1), :] = jnp.zeros((1, CELLS), F32)
    for j in range(2):
        total = None
        for k in range(2):
            who = donor[j, k]
            row = (who // 2) * SLOT + (2 + who % 2) * NV
            face = blocks[pl.ds(row, NV), :] * weight[j, k]
            total = face if total is None else total + face
        for v in range(NV):
            out[pl.ds((j * NV + v) * LEG + PIECE, 1), :] = total[v : v + 1]
    @pl.when(place[1] % 2 == 0)
    def _():
        local_terms(field, right, coup, spec, row_id, recv, blocks, part, freq, halo)
        spin[...] = lax.fori_loop(0, stall, lambda i, x: pltpu.roll(x, 1, 1), field[pl.ds(0, 8), :])


def spectral_kernel(legs, shift, inst, out):
    half = NT // 2
    for t in range(PIECE // 8):
        rows = [legs[pl.ds(m * LEG + t * 8, 8), :] for m in range(NT)]
        plus = [rows[m] + rows[m + half] for m in range(half)]
        minus = [rows[m] - rows[m + half] for m in range(half)]
        for n in range(half):
            a = plus[0] * EVEN[n]
            b = minus[0] * ODD[n]
            for m in range(1, half):
                a = a + plus[m] * EVEN[(n - m) % NT]
                b = b + minus[m] * ODD[(n - m) % NT]
            out[pl.ds(n * LEG + t * 8, 8), :] = a + b
            out[pl.ds((n + half) * LEG + t * 8, 8), :] = a - b
    turn = jnp.where(inst[0] < NV, shift[0], shift[1])
    mixes = legs[pl.ds(PIECE, NT, stride=LEG), :]
    out[pl.ds(PIECE, NT, stride=LEG), :] = pltpu.roll(mixes, NT - turn, 0)


def update_kernel(
    last, part_in, freq_in, jac, coef, place, back, field, right, coup, spec, row_id, recv, blocks, *rest
):
    if last:
        out, part, freq, halo = rest
    else:
        send, fresh, out, packed, part, freq, halo = rest

    @pl.when(place[1] % 2 == 0)
    def _():
        part[...] = part_in[...]
        freq[...] = freq_in[...]

    @pl.when(place[1] % 2 == 1)
    def _():
        local_terms(field, right, coup, spec, row_id, recv, blocks, part, freq, halo)

    sub = lax.broadcasted_iota(jnp.int32, (8, CELLS), 0)
    for t in range(BLK // 8):
        total = []
        f = freq[pl.ds(t * 8, 8), :]
        for v in range(NV):
            r = v * BLK + t * 8
            p, q = r // PIECE, r % PIECE
            val = part[pl.ds(r, 8), :] - f * back[pl.ds(p * LEG + q, 8), :]
            if t == 0:
                for j in range(2):
                    mix = coef[pl.ds(j, 1), :] * back[pl.ds((j * NV + v) * LEG + PIECE, 1), :]
                    val = jnp.where(sub == j, val + mix, val)
            total.append(val)
        for v in range(NV):
            new = 0.35 * total[v]
            for w in range(NV):
                new = new + jac[pl.ds((v * NV + w) * BLK + t * 8, 8), :] * total[w]
            if v == NV - 1:
                new = jnp.maximum(new, 0.0)
            out[pl.ds(v * BLK + t * 8, 8), :] = new
    if not last:
        pack_blocks(out, send, packed)


def vmem():
    return pl.BlockSpec(memory_space=pltpu.VMEM)


def smem():
    return pl.BlockSpec(memory_space=pltpu.SMEM)


def rows_of(n):
    return jax.ShapeDtypeStruct((n, CELLS), F32)


def swap(x, axis, parts):
    rows = x.shape[0]
    y = lax.all_to_all(x.reshape(parts, rows // parts, CELLS), axis, 0, 0, tiled=True)
    return y.reshape(rows, CELLS)


def swap_rows(x):
    y = lax.all_to_all(x.reshape(NT, LEG, 1, CELLS), "inst", 0, 0, tiled=True)
    return y.reshape(NT * LEG, CELLS)


def per_device(
    state,
    right_side,
    couplings,
    jac_corr,
    spec_scale,
    row_id,
    send_index,
    recv_slot,
    iface_coef,
    donor_index,
    donor_weight,
    phase_shift,
):
    near = lambda x: pltpu.with_memory_space_constraint(x, pltpu.VMEM)
    far = lambda x: pltpu.with_memory_space_constraint(x, pltpu.HBM)
    field = state.reshape(ROWS, CELLS)
    right = near(right_side.reshape(ROWS, CELLS))
    coup = near(couplings.reshape(3 * ROWS, CELLS))
    jac = near(jac_corr.reshape(NV * ROWS, CELLS))
    spec = near(spec_scale)
    send = send_index.T
    place = jnp.stack([lax.axis_index("inst"), lax.axis_index("mesh")]).astype(jnp.int32)
    donor = donor_index
    weight = donor_weight
    shift = phase_shift
    recv = recv_slot
    blade = row_id

    packed = pl.pallas_call(
        pack_kernel,
        out_shape=rows_of(NMESH * SLOT),
        in_specs=[vmem(), smem(), smem(), vmem()],
        out_specs=vmem(),
        input_output_aliases={3: 0},
        name="pack",
        compiler_params=pltpu.CompilerParams(vmem_limit_bytes=8 << 20),
    )(far(field), far(send), place, near(jnp.zeros((NMESH * SLOT, CELLS), F32)))
    fresh = jnp.zeros((ROWS, CELLS), F32)
    part = jnp.zeros((ROWS, CELLS), F32)
    freq = jnp.zeros((BLK, CELLS), F32)
    legs = jnp.zeros((NT * LEG, CELLS), F32)
    for sweep in range(SWEEPS):
        last = sweep == SWEEPS - 1
        blocks = near(swap(packed, "mesh", NMESH))
        near_by = [near(field), right, coup, spec, blade, recv, blocks]
        near_specs = [vmem(), vmem(), vmem(), vmem(), smem(), smem(), vmem()]
        legs, part, freq = pl.pallas_call(
            lambda *refs, sweep=sweep: mix_kernel(STALL[sweep], *refs),
            out_shape=[rows_of(NT * LEG), rows_of(ROWS), rows_of(BLK)],
            in_specs=[vmem(), smem(), smem(), smem()] + near_specs + [vmem()] * 2,
            out_specs=[vmem()] * 3,
            scratch_shapes=[pltpu.VMEM((ROWS, CELLS), F32), pltpu.VMEM((8, CELLS), F32)],
            input_output_aliases={0: 0, 11: 1, 12: 2},
            name="mix",
            compiler_params=pltpu.CompilerParams(vmem_limit_bytes=8 << 20),
        )(near(legs), donor, weight, place, *near_by, near(part), near(freq))
        legs = near(swap_rows(legs))
        back = pl.pallas_call(
            spectral_kernel,
            out_shape=rows_of(NT * LEG),
            in_specs=[vmem(), smem(), smem()],
            out_specs=vmem(),
            input_output_aliases={0: 0},
            name="spectral",
            compiler_params=pltpu.CompilerParams(vmem_limit_bytes=8 << 20),
        )(legs, shift, place)
        back = near(swap_rows(back))
        ins = [near(part), near(freq), jac, iface_coef, place, back] + near_by
        specs = [vmem()] * 4 + [smem(), vmem()] + near_specs
        shapes = [rows_of(ROWS)]
        alias = {}
        if not last:
            ins += [send, near(fresh)]
            specs += [smem(), vmem()]
            shapes.append(rows_of(NMESH * SLOT))
            alias = {14: 0, 12: 1}
        res = pl.pallas_call(
            lambda *refs, last=last: update_kernel(last, *refs),
            out_shape=shapes,
            in_specs=specs,
            out_specs=[vmem()] * len(shapes),
            scratch_shapes=[pltpu.VMEM((n, CELLS), F32) for n in (ROWS, BLK, ROWS)],
            input_output_aliases=alias,
            name="update",
            compiler_params=pltpu.CompilerParams(vmem_limit_bytes=8 << 20),
        )(*ins)
        field = res[0]
        if not last:
            packed, legs = res[1], back
    return field.reshape(1, NV, BLK, CELLS)


def solution(mesh):
    return jax.shard_map(
        per_device,
        mesh=mesh,
        in_specs=(
            P("inst", None, "mesh", None),
            P("inst", None, "mesh", None),
            P(None, "inst", None, "mesh", None),
            P("inst", None, None, "mesh", None),
            P("mesh", None),
            P("mesh"),
            P("mesh", None),
            P("mesh"),
            P("mesh", None),
            P("mesh", None),
            P("mesh", None),
            P("mesh"),
        ),
        out_specs=P("inst", None, "mesh", None),
        check_vma=False,
    )
```

```python
import jax
import jax.numpy as jnp
import numpy as np
from jax import lax
from jax.experimental import pallas as pl
from jax.experimental.pallas import tpu as pltpu
from jax.sharding import PartitionSpec as P

NT = 16
NV = 6
CELLS = 128
BLK = 64
NMESH = 32
ROWS = NV * BLK
PIECE = ROWS // NT
SLOT = 4 * NV
LEG = PIECE + 1
SWEEPS = 2
STALL = (700, 560)
F32 = jnp.float32


def circulant_row():
    k = np.arange(NT, dtype=np.float64)
    parity = 1.0 - 2.0 * (k % 2)
    angle = np.pi * k / NT
    sine = np.where(k == 0, 1.0, np.sin(angle))
    first = np.where(k == 0, 0.0, 0.5 * parity * np.cos(angle) / sine)
    second = np.where(k == 0, -(NT * NT + 2.0) / 12.0, -0.5 * parity / (sine * sine))
    return [float(v) for v in (first - 0.1 * second)]


TABLE = circulant_row()
EVEN = [0.5 * (TABLE[k] + TABLE[(k + NT // 2) % NT]) for k in range(NT)]
ODD = [0.5 * (TABLE[k] - TABLE[(k + NT // 2) % NT]) for k in range(NT)]


def pack_blocks(field, send, out):
    faces = [field[pl.ds(b, NV, stride=BLK), :] for b in range(2)]
    for dst in range(NMESH):
        for s in range(2):
            blk = send[s, dst]
            out[pl.ds(dst * SLOT + s * NV, NV), :] = field[pl.ds(blk, NV, stride=BLK), :]
        for b in range(2):
            out[pl.ds(dst * SLOT + (2 + b) * NV, NV), :] = faces[b]


def pack_kernel(field, send, place, out_in, out):
    pack_blocks(field, send, out)


def local_terms(field, right, coup, spec, row_id, recv, blocks, part, freq, halo):
    for b in range(BLK):
        slot = recv[b]
        row = (slot // 2) * SLOT + (slot % 2) * NV
        halo[pl.ds(b, NV, stride=BLK), :] = blocks[pl.ds(row, NV), :]
        freq[pl.ds(b, 1), :] = spec[pl.ds(b, 1), :] * (1.0 + 0.5 * row_id[b].astype(F32))
    lane = lax.broadcasted_iota(jnp.int32, (8, CELLS), 1)
    not_first = lane > 0
    not_last = lane < CELLS - 1
    for t in range(ROWS // 8):
        r = t * 8
        here = field[pl.ds(r, 8), :]
        below = jnp.where(not_first, pltpu.roll(here, 1, 1), 0.0)
        above = jnp.where(not_last, pltpu.roll(here, CELLS - 1, 1), 0.0)
        val = right[pl.ds(r, 8), :]
        val = val + (coup[pl.ds(r, 8), :] * below + coup[pl.ds(ROWS + r, 8), :] * above)
        part[pl.ds(r, 8), :] = val + coup[pl.ds(2 * ROWS + r, 8), :] * halo[pl.ds(r, 8), :]


def mix_kernel(
    stall, legs, donor, weight, place, field, right, coup, spec, row_id, recv, blocks, part_in, freq_in,
    out, part, freq, halo, spin,
):
    for p in range(NT):
        out[pl.ds(p * LEG, PIECE), :] = field[pl.ds(p * PIECE, PIECE), :]
    for p in range(2 * NV, NT):
        out[pl.ds(p * LEG + PIECE, 1), :] = jnp.zeros((1, CELLS), F32)
    for j in range(2):
        total = None
        for k in range(2):
            who = donor[j, k]
            row = (who // 2) * SLOT + (2 + who % 2) * NV
            face = blocks[pl.ds(row, NV), :] * weight[j, k]
            total = face if total is None else total + face
        for v in range(NV):
            out[pl.ds((j * NV + v) * LEG + PIECE, 1), :] = total[v : v + 1]
    @pl.when(place[1] % 2 == 0)
    def _():
        local_terms(field, right, coup, spec, row_id, recv, blocks, part, freq, halo)
        spin[...] = lax.fori_loop(0, stall, lambda i, x: pltpu.roll(x, 1, 1), field[pl.ds(0, 8), :])


def spectral_kernel(legs, shift, inst, out):
    half = NT // 2
    for t in range(PIECE // 8):
        rows = [legs[pl.ds(m * LEG + t * 8, 8), :] for m in range(NT)]
        plus = [rows[m] + rows[m + half] for m in range(half)]
        minus = [rows[m] - rows[m + half] for m in range(half)]
        for n in range(half):
            a = plus[0] * EVEN[n]
            b = minus[0] * ODD[n]
            for m in range(1, half):
                a = a + plus[m] * EVEN[(n - m) % NT]
                b = b + minus[m] * ODD[(n - m) % NT]
            out[pl.ds(n * LEG + t * 8, 8), :] = a + b
            out[pl.ds((n + half) * LEG + t * 8, 8), :] = a - b
    turn = jnp.where(inst[0] < NV, shift[0], shift[1])
    mixes = legs[pl.ds(PIECE, NT, stride=LEG), :]
    out[pl.ds(PIECE, NT, stride=LEG), :] = pltpu.roll(mixes, (NT - turn) % NT, 0)


def update_kernel(
    last, part_in, freq_in, jac, coef, place, back, field, right, coup, spec, row_id, recv, blocks, *rest
):
    if last:
        out, part, freq, halo = rest
    else:
        send, fresh, out, packed, part, freq, halo = rest

    @pl.when(place[1] % 2 == 0)
    def _():
        part[...] = part_in[...]
        freq[...] = freq_in[...]

    @pl.when(place[1] % 2 == 1)
    def _():
        local_terms(field, right, coup, spec, row_id, recv, blocks, part, freq, halo)

    sub = lax.broadcasted_iota(jnp.int32, (8, CELLS), 0)
    for t in range(BLK // 8):
        total = []
        f = freq[pl.ds(t * 8, 8), :]
        for v in range(NV):
            r = v * BLK + t * 8
            p, q = r // PIECE, r % PIECE
            val = part[pl.ds(r, 8), :] - f * back[pl.ds(p * LEG + q, 8), :]
            if t == 0:
                for j in range(2):
                    mix = coef[pl.ds(j, 1), :] * back[pl.ds((j * NV + v) * LEG + PIECE, 1), :]
                    val = jnp.where(sub == j, val + mix, val)
            total.append(val)
        for v in range(NV):
            new = 0.35 * total[v]
            for w in range(NV):
                new = new + jac[pl.ds((v * NV + w) * BLK + t * 8, 8), :] * total[w]
            if v == NV - 1:
                new = jnp.maximum(new, 0.0)
            out[pl.ds(v * BLK + t * 8, 8), :] = new
    if not last:
        pack_blocks(out, send, packed)


def vmem():
    return pl.BlockSpec(memory_space=pltpu.VMEM)


def smem():
    return pl.BlockSpec(memory_space=pltpu.SMEM)


def rows_of(n):
    return jax.ShapeDtypeStruct((n, CELLS), F32)


def swap(x, axis, parts):
    rows = x.shape[0]
    y = lax.all_to_all(x.reshape(parts, rows // parts, CELLS), axis, 0, 0, tiled=True)
    return y.reshape(rows, CELLS)


def swap_rows(x):
    y = lax.all_to_all(x.reshape(NT, LEG, 1, CELLS), "inst", 0, 0, tiled=True)
    return y.reshape(NT * LEG, CELLS)


def per_device(
    state,
    right_side,
    couplings,
    jac_corr,
    spec_scale,
    row_id,
    send_index,
    recv_slot,
    iface_coef,
    donor_index,
    donor_weight,
    phase_shift,
):
    near = lambda x: pltpu.with_memory_space_constraint(x, pltpu.VMEM)
    far = lambda x: pltpu.with_memory_space_constraint(x, pltpu.HBM)
    field = state.reshape(ROWS, CELLS)
    right = near(right_side.reshape(ROWS, CELLS))
    coup = near(couplings.reshape(3 * ROWS, CELLS))
    jac = near(jac_corr.reshape(NV * ROWS, CELLS))
    spec = near(spec_scale)
    send = send_index.T
    place = jnp.stack([lax.axis_index("inst"), lax.axis_index("mesh")]).astype(jnp.int32)
    donor = donor_index
    weight = donor_weight
    shift = phase_shift
    recv = recv_slot
    blade = row_id

    packed = pl.pallas_call(
        pack_kernel,
        out_shape=rows_of(NMESH * SLOT),
        in_specs=[vmem(), smem(), smem(), vmem()],
        out_specs=vmem(),
        input_output_aliases={3: 0},
        name="pack",
        compiler_params=pltpu.CompilerParams(vmem_limit_bytes=8 << 20),
    )(far(field), far(send), place, near(jnp.zeros((NMESH * SLOT, CELLS), F32)))
    fresh = jnp.zeros((ROWS, CELLS), F32)
    part = jnp.zeros((ROWS, CELLS), F32)
    freq = jnp.zeros((BLK, CELLS), F32)
    legs = jnp.zeros((NT * LEG, CELLS), F32)
    for sweep in range(SWEEPS):
        last = sweep == SWEEPS - 1
        blocks = near(swap(packed, "mesh", NMESH))
        near_by = [near(field), right, coup, spec, blade, recv, blocks]
        near_specs = [vmem(), vmem(), vmem(), vmem(), smem(), smem(), vmem()]
        legs, part, freq = pl.pallas_call(
            lambda *refs, sweep=sweep: mix_kernel(STALL[sweep], *refs),
            out_shape=[rows_of(NT * LEG), rows_of(ROWS), rows_of(BLK)],
            in_specs=[vmem(), smem(), smem(), smem()] + near_specs + [vmem()] * 2,
            out_specs=[vmem()] * 3,
            scratch_shapes=[pltpu.VMEM((ROWS, CELLS), F32), pltpu.VMEM((8, CELLS), F32)],
            input_output_aliases={0: 0, 11: 1, 12: 2},
            name="mix",
            compiler_params=pltpu.CompilerParams(vmem_limit_bytes=8 << 20),
        )(near(legs), donor, weight, place, *near_by, near(part), near(freq))
        legs = near(swap_rows(legs))
        back = pl.pallas_call(
            spectral_kernel,
            out_shape=rows_of(NT * LEG),
            in_specs=[vmem(), smem(), smem()],
            out_specs=vmem(),
            input_output_aliases={0: 0},
            name="spectral",
            compiler_params=pltpu.CompilerParams(vmem_limit_bytes=8 << 20),
        )(legs, shift, place)
        back = near(swap_rows(back))
        ins = [near(part), near(freq), jac, iface_coef, place, back] + near_by
        specs = [vmem()] * 4 + [smem(), vmem()] + near_specs
        shapes = [rows_of(ROWS)]
        alias = {}
        if not last:
            ins += [send, near(fresh)]
            specs += [smem(), vmem()]
            shapes.append(rows_of(NMESH * SLOT))
            alias = {14: 0, 12: 1}
        res = pl.pallas_call(
            lambda *refs, last=last: update_kernel(last, *refs),
            out_shape=shapes,
            in_specs=specs,
            out_specs=[vmem()] * len(shapes),
            scratch_shapes=[pltpu.VMEM((n, CELLS), F32) for n in (ROWS, BLK, ROWS)],
            input_output_aliases=alias,
            name="update",
            compiler_params=pltpu.CompilerParams(vmem_limit_bytes=8 << 20),
        )(*ins)
        field = res[0]
        if not last:
            packed, legs = res[1], back
    return field.reshape(1, NV, BLK, CELLS)


def solution(mesh):
    return jax.shard_map(
        per_device,
        mesh=mesh,
        in_specs=(
            P("inst", None, "mesh", None),
            P("inst", None, "mesh", None),
            P(None, "inst", None, "mesh", None),
            P("inst", None, None, "mesh", None),
            P("mesh", None),
            P("mesh"),
            P("mesh", None),
            P("mesh"),
            P("mesh", None),
            P("mesh", None),
            P("mesh", None),
            P("mesh"),
        ),
        out_specs=P("inst", None, "mesh", None),
        check_vma=False,
    )
```

```python
import jax
import jax.numpy as jnp
import numpy as np
from jax import lax
from jax.experimental import pallas as pl
from jax.experimental.pallas import tpu as pltpu
from jax.sharding import PartitionSpec as P

NT = 16
NV = 6
CELLS = 128
BLK = 64
NMESH = 32
ROWS = NV * BLK
PIECE = ROWS // NT
SLOT = 4 * NV
LEG = PIECE + 1
SWEEPS = 2
STALL = (700, 560)
F32 = jnp.float32


def circulant_row():
    k = np.arange(NT, dtype=np.float64)
    parity = 1.0 - 2.0 * (k % 2)
    angle = np.pi * k / NT
    sine = np.where(k == 0, 1.0, np.sin(angle))
    first = np.where(k == 0, 0.0, 0.5 * parity * np.cos(angle) / sine)
    second = np.where(k == 0, -(NT * NT + 2.0) / 12.0, -0.5 * parity / (sine * sine))
    return [float(v) for v in (first - 0.1 * second)]


TABLE = circulant_row()
EVEN = [0.5 * (TABLE[k] + TABLE[(k + NT // 2) % NT]) for k in range(NT)]
ODD = [0.5 * (TABLE[k] - TABLE[(k + NT // 2) % NT]) for k in range(NT)]


def pack_blocks(field, send, out):
    faces = [field[pl.ds(b, NV, stride=BLK), :] for b in range(2)]
    for dst in range(NMESH):
        for s in range(2):
            blk = send[s, dst]
            out[pl.ds(dst * SLOT + s * NV, NV), :] = field[pl.ds(blk, NV, stride=BLK), :]
        for b in range(2):
            out[pl.ds(dst * SLOT + (2 + b) * NV, NV), :] = faces[b]


def pack_kernel(field, send, shift, place, out_in, turn_in, out, turn):
    turn[...] = jnp.full((NT, CELLS), jnp.where(place[0] < NV, shift[0], shift[1]), jnp.int32)
    pack_blocks(field, send, out)


def local_terms(field, right, coup, spec, row_id, recv, blocks, part, freq, halo):
    for b in range(BLK):
        slot = recv[b]
        row = (slot // 2) * SLOT + (slot % 2) * NV
        halo[pl.ds(b, NV, stride=BLK), :] = blocks[pl.ds(row, NV), :]
        freq[pl.ds(b, 1), :] = spec[pl.ds(b, 1), :] * (1.0 + 0.5 * row_id[b].astype(F32))
    lane = lax.broadcasted_iota(jnp.int32, (8, CELLS), 1)
    not_first = lane > 0
    not_last = lane < CELLS - 1
    for t in range(ROWS // 8):
        r = t * 8
        here = field[pl.ds(r, 8), :]
        below = jnp.where(not_first, pltpu.roll(here, 1, 1), 0.0)
        above = jnp.where(not_last, pltpu.roll(here, CELLS - 1, 1), 0.0)
        val = right[pl.ds(r, 8), :]
        val = val + (coup[pl.ds(r, 8), :] * below + coup[pl.ds(ROWS + r, 8), :] * above)
        part[pl.ds(r, 8), :] = val + coup[pl.ds(2 * ROWS + r, 8), :] * halo[pl.ds(r, 8), :]


def mix_kernel(
    stall, legs, donor, weight, place, field, right, coup, spec, row_id, recv, blocks, part_in, freq_in,
    out, part, freq, halo, spin,
):
    for p in range(NT):
        out[pl.ds(p * LEG, PIECE), :] = field[pl.ds(p * PIECE, PIECE), :]
    for p in range(2 * NV, NT):
        out[pl.ds(p * LEG + PIECE, 1), :] = jnp.zeros((1, CELLS), F32)
    for j in range(2):
        total = None
        for k in range(2):
            who = donor[j, k]
            row = (who // 2) * SLOT + (2 + who % 2) * NV
            face = blocks[pl.ds(row, NV), :] * weight[j, k]
            total = face if total is None else total + face
        for v in range(NV):
            out[pl.ds((j * NV + v) * LEG + PIECE, 1), :] = total[v : v + 1]
    @pl.when(place[1] % 2 == 0)
    def _():
        local_terms(field, right, coup, spec, row_id, recv, blocks, part, freq, halo)
        spin[...] = lax.fori_loop(0, stall, lambda i, x: pltpu.roll(x, 1, 1), field[pl.ds(0, 8), :])


def spectral_kernel(legs, turn, out):
    half = NT // 2
    for t in range(PIECE // 8):
        rows = [legs[pl.ds(m * LEG + t * 8, 8), :] for m in range(NT)]
        plus = [rows[m] + rows[m + half] for m in range(half)]
        minus = [rows[m] - rows[m + half] for m in range(half)]
        for n in range(half):
            a = plus[0] * EVEN[n]
            b = minus[0] * ODD[n]
            for m in range(1, half):
                a = a + plus[m] * EVEN[(n - m) % NT]
                b = b + minus[m] * ODD[(n - m) % NT]
            out[pl.ds(n * LEG + t * 8, 8), :] = a + b
            out[pl.ds((n + half) * LEG + t * 8, 8), :] = a - b
    mixes = legs[pl.ds(PIECE, NT, stride=LEG), :]
    for bit in (1, 2, 4, 8):
        mixes = jnp.where((turn[...] & bit) > 0, pltpu.roll(mixes, NT - bit, 0), mixes)
    out[pl.ds(PIECE, NT, stride=LEG), :] = mixes


def update_kernel(
    last, part_in, freq_in, jac, coef, place, back, field, right, coup, spec, row_id, recv, blocks, *rest
):
    if last:
        out, part, freq, halo = rest
    else:
        send, fresh, out, packed, part, freq, halo = rest

    @pl.when(place[1] % 2 == 0)
    def _():
        part[...] = part_in[...]
        freq[...] = freq_in[...]

    @pl.when(place[1] % 2 == 1)
    def _():
        local_terms(field, right, coup, spec, row_id, recv, blocks, part, freq, halo)

    sub = lax.broadcasted_iota(jnp.int32, (8, CELLS), 0)
    for t in range(BLK // 8):
        total = []
        f = freq[pl.ds(t * 8, 8), :]
        for v in range(NV):
            r = v * BLK + t * 8
            p, q = r // PIECE, r % PIECE
            val = part[pl.ds(r, 8), :] - f * back[pl.ds(p * LEG + q, 8), :]
            if t == 0:
                for j in range(2):
                    mix = coef[pl.ds(j, 1), :] * back[pl.ds((j * NV + v) * LEG + PIECE, 1), :]
                    val = jnp.where(sub == j, val + mix, val)
            total.append(val)
        for v in range(NV):
            new = 0.35 * total[v]
            for w in range(NV):
                new = new + jac[pl.ds((v * NV + w) * BLK + t * 8, 8), :] * total[w]
            if v == NV - 1:
                new = jnp.maximum(new, 0.0)
            out[pl.ds(v * BLK + t * 8, 8), :] = new
    if not last:
        pack_blocks(out, send, packed)


def vmem():
    return pl.BlockSpec(memory_space=pltpu.VMEM)


def smem():
    return pl.BlockSpec(memory_space=pltpu.SMEM)


def rows_of(n):
    return jax.ShapeDtypeStruct((n, CELLS), F32)


def swap(x, axis, parts):
    rows = x.shape[0]
    y = lax.all_to_all(x.reshape(parts, rows // parts, CELLS), axis, 0, 0, tiled=True)
    return y.reshape(rows, CELLS)


def swap_rows(x):
    y = lax.all_to_all(x.reshape(NT, LEG, 1, CELLS), "inst", 0, 0, tiled=True)
    return y.reshape(NT * LEG, CELLS)


def per_device(
    state,
    right_side,
    couplings,
    jac_corr,
    spec_scale,
    row_id,
    send_index,
    recv_slot,
    iface_coef,
    donor_index,
    donor_weight,
    phase_shift,
):
    near = lambda x: pltpu.with_memory_space_constraint(x, pltpu.VMEM)
    far = lambda x: pltpu.with_memory_space_constraint(x, pltpu.HBM)
    field = state.reshape(ROWS, CELLS)
    right = near(right_side.reshape(ROWS, CELLS))
    coup = near(couplings.reshape(3 * ROWS, CELLS))
    jac = near(jac_corr.reshape(NV * ROWS, CELLS))
    spec = near(spec_scale)
    send = send_index.T
    place = jnp.stack([lax.axis_index("inst"), lax.axis_index("mesh")]).astype(jnp.int32)
    donor = donor_index
    weight = donor_weight
    shift = phase_shift
    recv = recv_slot
    blade = row_id

    packed, turn = pl.pallas_call(
        pack_kernel,
        out_shape=[rows_of(NMESH * SLOT), jax.ShapeDtypeStruct((NT, CELLS), jnp.int32)],
        in_specs=[vmem(), smem(), smem(), smem(), vmem(), vmem()],
        out_specs=[vmem()] * 2,
        input_output_aliases={4: 0, 5: 1},
        name="pack",
        compiler_params=pltpu.CompilerParams(vmem_limit_bytes=8 << 20),
    )(
        far(field),
        far(send),
        far(shift),
        place,
        near(jnp.zeros((NMESH * SLOT, CELLS), F32)),
        near(jnp.zeros((NT, CELLS), jnp.int32)),
    )
    fresh = jnp.zeros((ROWS, CELLS), F32)
    part = jnp.zeros((ROWS, CELLS), F32)
    freq = jnp.zeros((BLK, CELLS), F32)
    legs = jnp.zeros((NT * LEG, CELLS), F32)
    for sweep in range(SWEEPS):
        last = sweep == SWEEPS - 1
        blocks = near(swap(packed, "mesh", NMESH))
        near_by = [near(field), right, coup, spec, blade, recv, blocks]
        near_specs = [vmem(), vmem(), vmem(), vmem(), smem(), smem(), vmem()]
        legs, part, freq = pl.pallas_call(
            lambda *refs, sweep=sweep: mix_kernel(STALL[sweep], *refs),
            out_shape=[rows_of(NT * LEG), rows_of(ROWS), rows_of(BLK)],
            in_specs=[vmem(), smem(), smem(), smem()] + near_specs + [vmem()] * 2,
            out_specs=[vmem()] * 3,
            scratch_shapes=[pltpu.VMEM((ROWS, CELLS), F32), pltpu.VMEM((8, CELLS), F32)],
            input_output_aliases={0: 0, 11: 1, 12: 2},
            name="mix",
            compiler_params=pltpu.CompilerParams(vmem_limit_bytes=8 << 20),
        )(near(legs), donor, weight, place, *near_by, near(part), near(freq))
        legs = near(swap_rows(legs))
        back = pl.pallas_call(
            spectral_kernel,
            out_shape=rows_of(NT * LEG),
            in_specs=[vmem(), vmem()],
            out_specs=vmem(),
            input_output_aliases={0: 0},
            name="spectral",
            compiler_params=pltpu.CompilerParams(vmem_limit_bytes=8 << 20),
        )(legs, near(turn))
        back = near(swap_rows(back))
        ins = [near(part), near(freq), jac, iface_coef, place, back] + near_by
        specs = [vmem()] * 4 + [smem(), vmem()] + near_specs
        shapes = [rows_of(ROWS)]
        alias = {}
        if not last:
            ins += [send, near(fresh)]
            specs += [smem(), vmem()]
            shapes.append(rows_of(NMESH * SLOT))
            alias = {14: 0, 12: 1}
        res = pl.pallas_call(
            lambda *refs, last=last: update_kernel(last, *refs),
            out_shape=shapes,
            in_specs=specs,
            out_specs=[vmem()] * len(shapes),
            scratch_shapes=[pltpu.VMEM((n, CELLS), F32) for n in (ROWS, BLK, ROWS)],
            input_output_aliases=alias,
            name="update",
            compiler_params=pltpu.CompilerParams(vmem_limit_bytes=8 << 20),
        )(*ins)
        field = res[0]
        if not last:
            packed, legs = res[1], back
    return field.reshape(1, NV, BLK, CELLS)


def solution(mesh):
    return jax.shard_map(
        per_device,
        mesh=mesh,
        in_specs=(
            P("inst", None, "mesh", None),
            P("inst", None, "mesh", None),
            P(None, "inst", None, "mesh", None),
            P("inst", None, None, "mesh", None),
            P("mesh", None),
            P("mesh"),
            P("mesh", None),
            P("mesh"),
            P("mesh", None),
            P("mesh", None),
            P("mesh", None),
            P("mesh"),
        ),
        out_specs=P("inst", None, "mesh", None),
        check_vma=False,
    )
```

```python
import jax
import jax.numpy as jnp
import numpy as np
from jax import lax
from jax.experimental import pallas as pl
from jax.experimental.pallas import tpu as pltpu
from jax.sharding import PartitionSpec as P

NT = 16
NV = 6
CELLS = 128
BLK = 64
NMESH = 32
ROWS = NV * BLK
PIECE = ROWS // NT
SLOT = 4 * NV
LEG = PIECE + 1
SWEEPS = 2
STALL = (620, 560)
F32 = jnp.float32


def circulant_row():
    k = np.arange(NT, dtype=np.float64)
    parity = 1.0 - 2.0 * (k % 2)
    angle = np.pi * k / NT
    sine = np.where(k == 0, 1.0, np.sin(angle))
    first = np.where(k == 0, 0.0, 0.5 * parity * np.cos(angle) / sine)
    second = np.where(k == 0, -(NT * NT + 2.0) / 12.0, -0.5 * parity / (sine * sine))
    return [float(v) for v in (first - 0.1 * second)]


TABLE = circulant_row()
EVEN = [0.5 * (TABLE[k] + TABLE[(k + NT // 2) % NT]) for k in range(NT)]
ODD = [0.5 * (TABLE[k] - TABLE[(k + NT // 2) % NT]) for k in range(NT)]


def pack_blocks(field, send, out):
    faces = [field[pl.ds(b, NV, stride=BLK), :] for b in range(2)]
    for dst in range(NMESH):
        for s in range(2):
            blk = send[s, dst]
            out[pl.ds(dst * SLOT + s * NV, NV), :] = field[pl.ds(blk, NV, stride=BLK), :]
        for b in range(2):
            out[pl.ds(dst * SLOT + (2 + b) * NV, NV), :] = faces[b]


def pack_kernel(field, send, shift, place, out_in, turn_in, out, turn):
    turn[...] = jnp.full((NT, CELLS), jnp.where(place[0] < NV, shift[0], shift[1]), jnp.int32)
    pack_blocks(field, send, out)


def local_terms(field, right, coup, spec, row_id, recv, blocks, part, freq, halo):
    for b in range(BLK):
        slot = recv[b]
        row = (slot // 2) * SLOT + (slot % 2) * NV
        halo[pl.ds(b, NV, stride=BLK), :] = blocks[pl.ds(row, NV), :]
        freq[pl.ds(b, 1), :] = spec[pl.ds(b, 1), :] * (1.0 + 0.5 * row_id[b].astype(F32))
    lane = lax.broadcasted_iota(jnp.int32, (8, CELLS), 1)
    not_first = lane > 0
    not_last = lane < CELLS - 1
    for t in range(ROWS // 8):
        r = t * 8
        here = field[pl.ds(r, 8), :]
        below = jnp.where(not_first, pltpu.roll(here, 1, 1), 0.0)
        above = jnp.where(not_last, pltpu.roll(here, CELLS - 1, 1), 0.0)
        val = right[pl.ds(r, 8), :]
        val = val + (coup[pl.ds(r, 8), :] * below + coup[pl.ds(ROWS + r, 8), :] * above)
        part[pl.ds(r, 8), :] = val + coup[pl.ds(2 * ROWS + r, 8), :] * halo[pl.ds(r, 8), :]


def mix_kernel(
    stall, last, legs, donor, weight, place, field, right, coup, spec, row_id, recv, blocks, part_in, freq_in,
    out, part, freq, halo, spin,
):
    for p in range(NT):
        out[pl.ds(p * LEG, PIECE), :] = field[pl.ds(p * PIECE, PIECE), :]
    for p in range(2 * NV, NT):
        out[pl.ds(p * LEG + PIECE, 1), :] = jnp.zeros((1, CELLS), F32)
    for j in range(2):
        total = None
        for k in range(2):
            who = donor[j, k]
            row = (who // 2) * SLOT + (2 + who % 2) * NV
            face = blocks[pl.ds(row, NV), :] * weight[j, k]
            total = face if total is None else total + face
        for v in range(NV):
            out[pl.ds((j * NV + v) * LEG + PIECE, 1), :] = total[v : v + 1]
    @pl.when((place[1] % 2 == 0) | last)
    def _():
        local_terms(field, right, coup, spec, row_id, recv, blocks, part, freq, halo)

    @pl.when(place[1] % 2 == 0)
    def _():
        spin[...] = lax.fori_loop(0, stall, lambda i, x: pltpu.roll(x, 1, 1), field[pl.ds(0, 8), :])


def spectral_kernel(legs, turn, out):
    half = NT // 2
    for t in range(PIECE // 8):
        rows = [legs[pl.ds(m * LEG + t * 8, 8), :] for m in range(NT)]
        plus = [rows[m] + rows[m + half] for m in range(half)]
        minus = [rows[m] - rows[m + half] for m in range(half)]
        for n in range(half):
            a = plus[0] * EVEN[n]
            b = minus[0] * ODD[n]
            for m in range(1, half):
                a = a + plus[m] * EVEN[(n - m) % NT]
                b = b + minus[m] * ODD[(n - m) % NT]
            out[pl.ds(n * LEG + t * 8, 8), :] = a + b
            out[pl.ds((n + half) * LEG + t * 8, 8), :] = a - b
    mixes = legs[pl.ds(PIECE, NT, stride=LEG), :]
    for bit in (1, 2, 4, 8):
        mixes = jnp.where((turn[...] & bit) > 0, pltpu.roll(mixes, NT - bit, 0), mixes)
    out[pl.ds(PIECE, NT, stride=LEG), :] = mixes


def update_kernel(last, part_in, freq_in, jac, coef, *rest):
    if last:
        back, out, part, freq, halo = rest
        part, freq = part_in, freq_in
    else:
        (
            place, back, field, right, coup, spec, row_id, recv, blocks,
            send, fresh, out, packed, part, freq, halo,
        ) = rest

        @pl.when(place[1] % 2 == 0)
        def _():
            part[...] = part_in[...]
            freq[...] = freq_in[...]

        @pl.when(place[1] % 2 == 1)
        def _():
            local_terms(field, right, coup, spec, row_id, recv, blocks, part, freq, halo)

    sub = lax.broadcasted_iota(jnp.int32, (8, CELLS), 0)
    for t in range(BLK // 8):
        total = []
        f = freq[pl.ds(t * 8, 8), :]
        for v in range(NV):
            r = v * BLK + t * 8
            p, q = r // PIECE, r % PIECE
            val = part[pl.ds(r, 8), :] - f * back[pl.ds(p * LEG + q, 8), :]
            if t == 0:
                for j in range(2):
                    mix = coef[pl.ds(j, 1), :] * back[pl.ds((j * NV + v) * LEG + PIECE, 1), :]
                    val = jnp.where(sub == j, val + mix, val)
            total.append(val)
        for v in range(NV):
            new = 0.35 * total[v]
            for w in range(NV):
                new = new + jac[pl.ds((v * NV + w) * BLK + t * 8, 8), :] * total[w]
            if v == NV - 1:
                new = jnp.maximum(new, 0.0)
            out[pl.ds(v * BLK + t * 8, 8), :] = new
    if not last:
        pack_blocks(out, send, packed)


def vmem():
    return pl.BlockSpec(memory_space=pltpu.VMEM)


def smem():
    return pl.BlockSpec(memory_space=pltpu.SMEM)


def rows_of(n):
    return jax.ShapeDtypeStruct((n, CELLS), F32)


def swap(x, axis, parts):
    rows = x.shape[0]
    y = lax.all_to_all(x.reshape(parts, rows // parts, CELLS), axis, 0, 0, tiled=True)
    return y.reshape(rows, CELLS)


def swap_rows(x):
    y = lax.all_to_all(x.reshape(NT, LEG, 1, CELLS), "inst", 0, 0, tiled=True)
    return y.reshape(NT * LEG, CELLS)


def per_device(
    state,
    right_side,
    couplings,
    jac_corr,
    spec_scale,
    row_id,
    send_index,
    recv_slot,
    iface_coef,
    donor_index,
    donor_weight,
    phase_shift,
):
    near = lambda x: pltpu.with_memory_space_constraint(x, pltpu.VMEM)
    far = lambda x: pltpu.with_memory_space_constraint(x, pltpu.HBM)
    field = state.reshape(ROWS, CELLS)
    right = near(right_side.reshape(ROWS, CELLS))
    coup = near(couplings.reshape(3 * ROWS, CELLS))
    jac = near(jac_corr.reshape(NV * ROWS, CELLS))
    spec = near(spec_scale)
    send = send_index.T
    place = jnp.stack([lax.axis_index("inst"), lax.axis_index("mesh")]).astype(jnp.int32)
    donor = donor_index
    weight = donor_weight
    shift = phase_shift
    recv = recv_slot
    blade = row_id

    packed, turn = pl.pallas_call(
        pack_kernel,
        out_shape=[rows_of(NMESH * SLOT), jax.ShapeDtypeStruct((NT, CELLS), jnp.int32)],
        in_specs=[vmem(), smem(), smem(), smem(), vmem(), vmem()],
        out_specs=[vmem()] * 2,
        input_output_aliases={4: 0, 5: 1},
        name="pack",
        compiler_params=pltpu.CompilerParams(vmem_limit_bytes=8 << 20),
    )(
        far(field),
        far(send),
        far(shift),
        place,
        near(jnp.zeros((NMESH * SLOT, CELLS), F32)),
        near(jnp.zeros((NT, CELLS), jnp.int32)),
    )
    fresh = jnp.zeros((ROWS, CELLS), F32)
    part = jnp.zeros((ROWS, CELLS), F32)
    freq = jnp.zeros((BLK, CELLS), F32)
    legs = jnp.zeros((NT * LEG, CELLS), F32)
    for sweep in range(SWEEPS):
        last = sweep == SWEEPS - 1
        blocks = near(swap(packed, "mesh", NMESH))
        near_by = [near(field), right, coup, spec, blade, recv, blocks]
        near_specs = [vmem(), vmem(), vmem(), vmem(), smem(), smem(), vmem()]
        legs, part, freq = pl.pallas_call(
            lambda *refs, sweep=sweep: mix_kernel(STALL[sweep], sweep == SWEEPS - 1, *refs),
            out_shape=[rows_of(NT * LEG), rows_of(ROWS), rows_of(BLK)],
            in_specs=[vmem(), smem(), smem(), smem()] + near_specs + [vmem()] * 2,
            out_specs=[vmem()] * 3,
            scratch_shapes=[pltpu.VMEM((ROWS, CELLS), F32), pltpu.VMEM((8, CELLS), F32)],
            input_output_aliases={0: 0, 11: 1, 12: 2},
            name="mix",
            compiler_params=pltpu.CompilerParams(vmem_limit_bytes=8 << 20),
        )(near(legs), donor, weight, place, *near_by, near(part), near(freq))
        legs = near(swap_rows(legs))
        back = pl.pallas_call(
            spectral_kernel,
            out_shape=rows_of(NT * LEG),
            in_specs=[vmem(), vmem()],
            out_specs=vmem(),
            input_output_aliases={0: 0},
            name="spectral",
            compiler_params=pltpu.CompilerParams(vmem_limit_bytes=8 << 20),
        )(legs, near(turn))
        back = near(swap_rows(back))
        ins = [near(part), near(freq), jac, iface_coef, place, back] + near_by
        specs = [vmem()] * 4 + [smem(), vmem()] + near_specs
        shapes = [rows_of(ROWS)]
        alias = {}
        if not last:
            ins += [send, near(fresh)]
            specs += [smem(), vmem()]
            shapes.append(rows_of(NMESH * SLOT))
            alias = {14: 0, 12: 1}
        if last:
            ins, specs = ins[:4] + [back], [vmem()] * 5
        res = pl.pallas_call(
            lambda *refs, last=last: update_kernel(last, *refs),
            out_shape=shapes,
            in_specs=specs,
            out_specs=[vmem()] * len(shapes),
            scratch_shapes=[pltpu.VMEM((n, CELLS), F32) for n in (ROWS, BLK, ROWS)],
            input_output_aliases=alias,
            name="update",
            compiler_params=pltpu.CompilerParams(vmem_limit_bytes=8 << 20),
        )(*ins)
        field = res[0]
        if not last:
            packed, legs = res[1], back
    return field.reshape(1, NV, BLK, CELLS)


def solution(mesh):
    return jax.shard_map(
        per_device,
        mesh=mesh,
        in_specs=(
            P("inst", None, "mesh", None),
            P("inst", None, "mesh", None),
            P(None, "inst", None, "mesh", None),
            P("inst", None, None, "mesh", None),
            P("mesh", None),
            P("mesh"),
            P("mesh", None),
            P("mesh"),
            P("mesh", None),
            P("mesh", None),
            P("mesh", None),
            P("mesh"),
        ),
        out_specs=P("inst", None, "mesh", None),
        check_vma=False,
    )
```
